32 devices in a mesh: mom: 8 (over z, x), tm: 4 (over y, core).
Axes of the slice: x: 2, y: 2, z: 4, core: 2. Of those that a mesh axis runs over, the one named last changes fastest.
Arguments:
- new_rows: float32 [4, 256, 16, 512], P(None, 'mom', None, 'tm'), may hold values from -9 to 9
- history: float32 [3, 2, 256, 512, 512], P(None, None, 'mom', 'tm'), may hold values from -0.25 to 0.25
- momentum_map: int32 [256], replicated, may hold values from 0 to 255, each once
- step_index: int32 [1], replicated, may hold values from 0 to 999
- history_len: int32 [1], replicated, may hold values from 256 to 512
Outputs:
- advanced_rows: float32 [4, 256, 16, 512], P(None, 'mom', None, 'tm')
The draws below stay inside these ranges and needn't reach their ends.
Inputs may be any that keep to these rules, and one draw needn't show every extreme that they name: `momentum_map`: each number of 0 to 255 appears once.
All inputs are finite; a program needn't handle non-finite values.
Results may differ from the reference program's by a relative error of at most 0.0003.
Values sent between devices are 32-bit elements; how exact they have to be, the bound alone decides.
A program may use at most 256 MiB of HBM per device.

```python
import jax
import jax.numpy as jnp
from jax import lax

SIDE = 16
MOMENTA = 256
HIST = 512
ROWS = 16


def levels(rng, extent, pieces, low, largest):
    loudness, own = 1.0, jax.random.fold_in(rng, 6)
    for dim, shards_of in pieces:
        steps = jnp.exp(jax.random.uniform(jax.random.fold_in(own, dim), (shards_of,), jnp.float32, low / len(pieces), largest / len(pieces)))
        loudness = loudness * jnp.repeat(steps, extent[dim] // shards_of).reshape([-1 if axis == dim else 1 for axis in range(len(extent))])
    return loudness


def noise(rng, shape, spread, reach, split=(), kind=jnp.bfloat16):
    factor_of = levels(rng, shape, split, -0.22, 0.18) if split else 1.0
    array = jax.random.normal(rng, shape, jnp.float32) * spread * factor_of
    return jnp.minimum(jnp.maximum(array, -reach), reach).astype(kind)


def setup_inputs(seed: int = 0) -> dict:
    splits = jax.random.split(jax.random.key(seed), 6)
    return {
        "new_rows": noise(splits[0], (4, MOMENTA, ROWS, HIST), 1.5, 9.0, ((1, 8), (3, 4)), jnp.float32),
        "history": noise(splits[1], (3, 2, MOMENTA, HIST, HIST), HIST ** -0.5, 0.25, ((2, 8), (3, 4)), jnp.float32),
        "momentum_map": jax.random.permutation(splits[2], MOMENTA).astype(jnp.int32),
        "step_index": jax.random.randint(splits[3], (1,), 0, 1000).astype(jnp.int32),
        "history_len": jax.random.randint(splits[4], (1,), HIST // 2, HIST + 1).astype(jnp.int32),
    }


TIME_STEP = 0.2
COUPLING = 5.0
DRIVE_RATE = 0.3
PRECISE = lax.Precision.HIGHEST


def lattice_tables(momentum_map, side):
    mom_count = momentum_map.shape[0]
    sites = jnp.arange(mom_count, dtype=jnp.int32)
    mom_x = momentum_map // side
    mom_y = momentum_map % side
    site_x = sites // side
    site_y = sites % side
    winding = (site_x[:, None] * mom_x[None, :] + site_y[:, None] * mom_y[None, :]) % side
    phases = winding.astype(jnp.float32) * (2.0 * jnp.pi / side)
    return jnp.cos(phases), jnp.sin(phases)


def band_energy(own_map, row_times, side):
    wave_x = (own_map // side).astype(jnp.float32) * (2.0 * jnp.pi / side)
    wave_y = (own_map % side).astype(jnp.float32) * (2.0 * jnp.pi / side)
    drift = DRIVE_RATE * row_times
    return -2.0 * (jnp.cos(wave_x[:, None] + drift[None, :]) + jnp.cos(wave_y[:, None] + drift[None, :]))


def to_sites(cosine_table, sine_table, lattice):
    mom_count = lattice.shape[1]
    paired = lattice.reshape(2, 2, mom_count, lattice.shape[2])
    parts_re = paired[:, 0]
    parts_im = paired[:, 1]

    def apply_table(table, values):
        return jnp.einsum("rk,wkc->wrc", table, values, precision=PRECISE)

    site_re = (apply_table(cosine_table, parts_re) - apply_table(sine_table, parts_im)) / mom_count
    site_im = (apply_table(cosine_table, parts_im) + apply_table(sine_table, parts_re)) / mom_count
    return jnp.stack([site_re, site_im], axis=1).reshape(4, cosine_table.shape[0], lattice.shape[2])


def from_sites(cosine_table, sine_table, lattice):
    paired = lattice.reshape(2, 2, lattice.shape[1], lattice.shape[2])
    parts_re = paired[:, 0]
    parts_im = paired[:, 1]

    def apply_table(table, values):
        return jnp.einsum("rk,wrc->wkc", table, values, precision=PRECISE)

    mom_re = apply_table(cosine_table, parts_re) + apply_table(sine_table, parts_im)
    mom_im = apply_table(cosine_table, parts_im) - apply_table(sine_table, parts_re)
    return jnp.stack([mom_re, mom_im], axis=1).reshape(4, cosine_table.shape[1], lattice.shape[2])


def bubble_term(left_re, left_im, right_re, right_im):
    square_re = left_re * left_re - left_im * left_im
    square_im = 2.0 * left_re * left_im
    factor = -COUPLING * COUPLING
    return factor * (square_re * right_re + square_im * right_im), factor * (square_im * right_re - square_re * right_im)


def bubble(lattice):
    ret_re, ret_im, less_re, less_im = lattice[0], lattice[1], lattice[2], lattice[3]
    great_re = less_re + ret_re
    great_im = less_im + ret_im
    lesser_re, lesser_im = bubble_term(less_re, less_im, great_re, great_im)
    greater_re, greater_im = bubble_term(great_re, great_im, less_re, less_im)
    return jnp.stack([greater_re - lesser_re, greater_im - lesser_im, lesser_re, lesser_im])


def contract(energy_pair, stored_pair):
    product = jnp.einsum("akiu,bkus->abkis", energy_pair, stored_pair, precision=PRECISE)
    return product[0, 0] - product[1, 1], product[0, 1] + product[1, 0]


def memory_integral(self_energy, history):
    ret_ret = contract(self_energy[0:2], history[0])
    ret_less = contract(self_energy[0:2], history[1])
    less_adv = contract(self_energy[2:4], history[2])
    return TIME_STEP * jnp.stack([ret_ret[0], ret_ret[1], ret_less[0] + less_adv[0], ret_less[1] + less_adv[1]])


def rotate(total):
    return jnp.stack([total[1], -total[0], total[3], -total[2]])


def reference(new_rows, history, momentum_map, step_index, history_len):
    mom_count = new_rows.shape[1]
    row_count = new_rows.shape[2]
    time_count = new_rows.shape[3]
    cosine_table, sine_table = lattice_tables(momentum_map, SIDE)
    memory_mask = (jnp.arange(time_count, dtype=jnp.int32) < history_len[0]).astype(jnp.float32)
    first_times = step_index[0].astype(jnp.float32) + jnp.arange(row_count, dtype=jnp.int32).astype(jnp.float32)

    def slope(estimate, offset_steps):
        band = band_energy(momentum_map, (first_times + offset_steps) * TIME_STEP, SIDE)
        lattice = to_sites(cosine_table, sine_table, estimate.reshape(4, mom_count, row_count * time_count))
        self_energy = from_sites(cosine_table, sine_table, bubble(lattice))
        self_energy = self_energy.reshape(4, mom_count, row_count, time_count) * memory_mask
        integral = memory_integral(self_energy, history)
        return rotate(band[None, :, :, None] * estimate + integral)

    current = new_rows
    for time_step in range(2):
        slope_now = slope(current, float(time_step))
        estimate = current + TIME_STEP * slope_now
        for corrector in range(2):
            estimate = current + 0.5 * TIME_STEP * (slope_now + slope(estimate, float(time_step + 1)))
        current = estimate
    return current
```

```python
import functools

import jax
import jax.numpy as jnp
from jax import lax
from jax.experimental import pallas as pl
from jax.experimental.pallas import tpu as pltpu
from jax.sharding import PartitionSpec as P


SIDE = 16


TIME_STEP = 0.2
COUPLING = 5.0
DRIVE_RATE = 0.3
PRECISE = lax.Precision.HIGHEST


def lattice_tables(momentum_map, side):
    mom_count = momentum_map.shape[0]
    sites = jnp.arange(mom_count, dtype=jnp.int32)
    mom_x = momentum_map // side
    mom_y = momentum_map % side
    site_x = sites // side
    site_y = sites % side
    winding = (site_x[:, None] * mom_x[None, :] + site_y[:, None] * mom_y[None, :]) % side
    phases = winding.astype(jnp.float32) * (2.0 * jnp.pi / side)
    return (jnp.cos(phases), jnp.sin(phases))


def band_energy(own_map, row_times, side):
    wave_x = (own_map // side).astype(jnp.float32) * (2.0 * jnp.pi / side)
    wave_y = (own_map % side).astype(jnp.float32) * (2.0 * jnp.pi / side)
    drift = DRIVE_RATE * row_times
    return -2.0 * (
        jnp.cos(wave_x[:, None] + drift[None, :]) + jnp.cos(wave_y[:, None] + drift[None, :])
    )


def to_sites(cosine_table, sine_table, lattice):
    mom_count = lattice.shape[1]
    paired = lattice.reshape(2, 2, mom_count, lattice.shape[2])
    parts_re = paired[:, 0]
    parts_im = paired[:, 1]

    def apply_table(table, values):
        return jnp.einsum("rk,wkc->wrc", table, values, precision=PRECISE)

    site_re = (apply_table(cosine_table, parts_re) - apply_table(sine_table, parts_im)) / mom_count
    site_im = (apply_table(cosine_table, parts_im) + apply_table(sine_table, parts_re)) / mom_count
    return jnp.stack([site_re, site_im], axis=1).reshape(4, cosine_table.shape[0], lattice.shape[2])


def from_sites(cosine_table, sine_table, lattice):
    paired = lattice.reshape(2, 2, lattice.shape[1], lattice.shape[2])
    parts_re = paired[:, 0]
    parts_im = paired[:, 1]

    def apply_table(table, values):
        return jnp.einsum("rk,wrc->wkc", table, values, precision=PRECISE)

    mom_re = apply_table(cosine_table, parts_re) + apply_table(sine_table, parts_im)
    mom_im = apply_table(cosine_table, parts_im) - apply_table(sine_table, parts_re)
    return jnp.stack([mom_re, mom_im], axis=1).reshape(4, cosine_table.shape[1], lattice.shape[2])


def bubble_term(left_re, left_im, right_re, right_im):
    square_re = left_re * left_re - left_im * left_im
    square_im = 2.0 * left_re * left_im
    factor = -COUPLING * COUPLING
    return (
        factor * (square_re * right_re + square_im * right_im),
        factor * (square_im * right_re - square_re * right_im),
    )


def bubble(lattice):
    ret_re, ret_im, less_re, less_im = (lattice[0], lattice[1], lattice[2], lattice[3])
    great_re = less_re + ret_re
    great_im = less_im + ret_im
    lesser_re, lesser_im = bubble_term(less_re, less_im, great_re, great_im)
    greater_re, greater_im = bubble_term(great_re, great_im, less_re, less_im)
    return jnp.stack([greater_re - lesser_re, greater_im - lesser_im, lesser_re, lesser_im])


def contract(energy_pair, stored_pair):
    product = jnp.einsum("akiu,bkus->abkis", energy_pair, stored_pair, precision=PRECISE)
    return (product[0, 0] - product[1, 1], product[0, 1] + product[1, 0])


def memory_integral(self_energy, history):
    ret_ret = contract(self_energy[0:2], history[0])
    ret_less = contract(self_energy[0:2], history[1])
    less_adv = contract(self_energy[2:4], history[2])
    return TIME_STEP * jnp.stack(
        [ret_ret[0], ret_ret[1], ret_less[0] + less_adv[0], ret_less[1] + less_adv[1]]
    )


def rotate(total):
    return jnp.stack([total[1], -total[0], total[3], -total[2]])


def body(new_rows, history, momentum_map, step_index, history_len):
    own_count = new_rows.shape[1]
    row_count = new_rows.shape[2]
    time_count = new_rows.shape[3]
    cosine_table, sine_table = lattice_tables(momentum_map, SIDE)
    mom_start = lax.axis_index("mom") * own_count
    own_map = lax.dynamic_slice_in_dim(momentum_map, mom_start, own_count, 0)
    time_start = lax.axis_index("tm") * time_count
    positions = time_start + jnp.arange(time_count, dtype=jnp.int32)
    memory_mask = (positions < history_len[0]).astype(jnp.float32)
    first_times = step_index[0].astype(jnp.float32) + jnp.arange(row_count, dtype=jnp.int32).astype(
        jnp.float32
    )

    def slope(estimate, offset_steps):
        band = band_energy(own_map, (first_times + offset_steps) * TIME_STEP, SIDE)
        flattened = estimate.reshape(4, own_count, row_count * time_count)
        by_site = lax.all_to_all(flattened, "mom", split_axis=2, concat_axis=1, tiled=True)
        site_energy = from_sites(
            cosine_table, sine_table, bubble(to_sites(cosine_table, sine_table, by_site))
        )
        returned = lax.all_to_all(site_energy, "mom", split_axis=1, concat_axis=2, tiled=True)
        self_energy = returned.reshape(4, own_count, row_count, time_count)
        self_energy = self_energy * memory_mask
        partial_rows = memory_integral(self_energy, history)
        integral = lax.psum_scatter(partial_rows, "tm", scatter_dimension=3, tiled=True)
        return rotate(band[None, :, :, None] * estimate + integral)

    current = new_rows
    for time_step in range(2):
        slope_now = slope(current, float(time_step))
        estimate = current + TIME_STEP * slope_now
        for corrector in range(2):
            estimate = current + 0.5 * TIME_STEP * (
                slope_now + slope(estimate, float(time_step + 1))
            )
        current = estimate
    return current


MESH = pl.DeviceIdType.MESH


def halves(values):
    high = values.astype(jnp.bfloat16)
    return high, (values - high.astype(jnp.float32)).astype(jnp.bfloat16)


def product(left, right):
    return jnp.dot(left, right, preferred_element_type=jnp.float32)


def triple(left_high, left_low, right):
    right_high, right_low = halves(right)
    return (
        product(left_high, right_high)
        + product(left_high, right_low)
        + product(left_low, right_high)
    )


STEPS = 2
CORRECTORS = 2
CORE_LAG = 1
CHIP_LAG = 3


def steps_kernel(
    mom_size,
    slots,
    state_ref,
    band_ref,
    mask_ref,
    site_high,
    site_low,
    back_high,
    back_low,
    history_ref,
    now,
    base,
    first_slope,
    outgoing,
    gathered,
    energy,
    returned,
    partial,
    core_rows,
    chip_rows,
    stored,
    stored_sem,
    row_send,
    row_recv,
    energy_send,
    energy_recv,
    core_send,
    core_recv,
    chip_send,
    chip_recv,
):
    mom = lax.axis_index("mom")
    tm = lax.axis_index("tm")
    core = tm % 2
    chip = tm // 2
    near = chip * 2 + (1 - core)
    far = (1 - chip) * 2 + core
    groups, _, pieces, _, chunk, times = outgoing.shape
    own = pieces * chunk
    rows = groups * mom_size
    sites = own * mom_size
    turns = groups * pieces
    stages = CORRECTORS + 1
    rounds = STEPS * stages
    fetches = rounds * groups * own

    def fetch(count):
        slot = count % slots
        return pltpu.make_async_copy(
            history_ref.at[:, :, count % own], stored.at[slot], stored_sem.at[slot]
        )

    @pl.loop(0, slots)
    def _(count):
        fetch(count).start()

    barrier = pltpu.get_barrier_semaphore()
    for step in range(1, mom_size):
        pl.semaphore_signal(
            barrier, inc=1, device_id={"mom": (mom + step) % mom_size}, device_id_type=MESH
        )
    for peer in (near, far):
        pl.semaphore_signal(barrier, inc=1, device_id={"tm": peer}, device_id_type=MESH)

    def peer_of(step):
        return (mom + step) % mom_size

    def row_copy(group, piece, step):
        return pltpu.make_async_remote_copy(
            src_ref=outgoing.at[group, peer_of(step), piece],
            dst_ref=gathered.at[group, mom, piece],
            send_sem=row_send.at[group, step],
            recv_sem=row_recv.at[group, step],
            device_id={"mom": peer_of(step)},
            device_id_type=MESH,
        )

    def all_rows(group, step):
        return pltpu.make_async_remote_copy(
            src_ref=outgoing.at[group, peer_of(step)],
            dst_ref=gathered.at[group, mom],
            send_sem=row_send.at[group, step],
            recv_sem=row_recv.at[group, step],
            device_id={"mom": peer_of(step)},
            device_id_type=MESH,
        )

    def landing(group, piece):
        depth = 4 * chunk
        start = ((group * pieces + piece) * mom_size + mom) * depth
        return pl.ds(pl.multiple_of(start, depth), depth)

    def energy_copy(group, piece, step):
        return pltpu.make_async_remote_copy(
            src_ref=energy.at[group, peer_of(step), piece],
            dst_ref=returned.at[landing(group, piece)],
            send_sem=energy_send.at[group, piece, step],
            recv_sem=energy_recv.at[group, piece, step],
            device_id={"mom": peer_of(step)},
            device_id_type=MESH,
        )

    def core_copy(parity, turn):
        return pltpu.make_async_remote_copy(
            src_ref=partial.at[turn, :, 1 - core],
            dst_ref=core_rows.at[parity, turn],
            send_sem=core_send.at[turn],
            recv_sem=core_recv.at[parity, turn],
            device_id={"tm": near},
            device_id_type=MESH,
        )

    def chip_copy(parity, turn):
        return pltpu.make_async_remote_copy(
            src_ref=partial.at[turn, 1 - chip, core],
            dst_ref=chip_rows.at[parity, turn],
            send_sem=chip_send.at[turn],
            recv_sem=chip_recv.at[parity, turn],
            device_id={"tm": far},
            device_id_type=MESH,
        )

    def publish(group, piece):
        for part in range(4):
            for row in range(mom_size):
                start = (part * own + piece * chunk) * rows + group * mom_size + row
                outgoing[group, row, piece, part] = now[pl.ds(start, chunk, stride=rows), :]
        gathered[group, mom, piece] = outgoing[group, mom, piece]

    def send_rows(group, piece):
        for step in range(1, mom_size):
            row_copy(group, piece, step).start()

    now[...] = state_ref[...]

    @pl.loop(0, turns)
    def _(turn):
        publish(turn // pieces, turn % pieces)

    pl.semaphore_wait(barrier, mom_size + 1)

    @pl.loop(0, turns)
    def _(turn):
        send_rows(turn // pieces, turn % pieces)

    mask = mask_ref[0:1, :]

    def site_stage(group):
        for step in range(1, mom_size):
            all_rows(group, step).wait_recv()
        fields = []
        for pair in range(2):
            both = jnp.concatenate(
                [gathered[group, :, :, 2 * pair + part].reshape(sites, times) for part in range(2)],
                axis=1,
            )
            turned = triple(site_high[...], site_low[...], both)
            fields.append((turned[:sites, :times] - turned[sites:, times:]) / sites)
            fields.append((turned[:sites, times:] + turned[sites:, :times]) / sites)
        ret_re, ret_im, less_re, less_im = fields
        great_re = less_re + ret_re
        great_im = less_im + ret_im
        lesser_re, lesser_im = bubble_term(less_re, less_im, great_re, great_im)
        greater_re, greater_im = bubble_term(great_re, great_im, less_re, less_im)
        pairs = (
            (greater_re - lesser_re, greater_im - lesser_im),
            (lesser_re, lesser_im),
        )
        for pair, (part_re, part_im) in enumerate(pairs):
            both = jnp.concatenate([part_re, part_im], axis=1)
            turned = triple(back_high[...], back_low[...], both)
            mom_re = (turned[:sites, :times] + turned[sites:, times:]) * mask
            mom_im = (turned[:sites, times:] - turned[sites:, :times]) * mask
            for part, values in ((2 * pair, mom_re), (2 * pair + 1, mom_im)):
                window = pl.ds(part * chunk, chunk)
                energy[group, :, :, window] = values.reshape(mom_size, pieces, chunk, times)

        @pl.loop(0, pieces)
        def _(piece):
            for step in range(1, mom_size):
                energy_copy(group, piece, step).start()
            returned[landing(group, piece)] = energy[group, mom, piece]

        for step in range(1, mom_size):
            all_rows(group, step).wait_send()

    def one_momentum(count, turn, inner):
        slot = count % slots
        fetch(count).wait()
        depth = 4 * chunk
        start = turn * mom_size * depth + inner
        ret_re, ret_im, less_re, less_im = [
            returned[pl.ds(start + part * chunk, mom_size, stride=depth), :] for part in range(4)
        ]
        lines = 2 * mom_size

        def folded(part_re, part_im):
            return jnp.concatenate(
                [
                    jnp.concatenate([part_re, -part_im], axis=1),
                    jnp.concatenate([part_im, part_re], axis=1),
                ],
                axis=0,
            )

        def applied(high, both, kind):
            weights_high, weights_low = halves(stored[slot, kind].reshape(2 * times, -1))
            stacked = product(both, weights_high)
            return stacked[:lines] + stacked[lines:] + product(high, weights_low)

        ret_high, ret_low = halves(folded(ret_re, ret_im))
        ret_both = jnp.concatenate([ret_high, ret_low], axis=0)
        less_high, less_low = halves(folded(less_re, less_im))
        less_both = jnp.concatenate([less_high, less_low], axis=0)
        ret_sum = applied(ret_high, ret_both, 0)
        less_sum = applied(ret_high, ret_both, 1) + applied(less_high, less_both, 2)
        for block in range(4):
            window = slice(block * times, (block + 1) * times)
            partial[turn, block // 2, block % 2, inner, :lines] = ret_sum[:, window]
            partial[turn, block // 2, block % 2, inner, lines:] = less_sum[:, window]

        @pl.when(count + slots < fetches)
        def _():
            fetch(count + slots).start()

    def update(parity, turn, inner, moment, first):
        group = turn // pieces
        index = (turn % pieces) * chunk + inner
        total = (
            partial[turn, chip, core, inner]
            + core_rows[parity, turn, chip, inner]
            + chip_rows[parity, turn, inner]
        )
        span = [
            pl.ds(
                pl.multiple_of((part * own + index) * rows + group * mom_size, mom_size), mom_size
            )
            for part in range(4)
        ]
        band = band_ref[
            pl.ds(
                pl.multiple_of((moment * own + index) * rows + group * mom_size, mom_size), mom_size
            ),
            :,
        ]
        terms = [
            band * now[span[part], :] + TIME_STEP * total[part * mom_size : (part + 1) * mom_size]
            for part in range(4)
        ]
        slopes = (terms[1], -terms[0], terms[3], -terms[2])
        for part in range(4):
            start = jnp.where(first, now[span[part], :], base[span[part], :])
            early = jnp.where(first, slopes[part], first_slope[span[part], :])
            base[span[part], :] = start
            first_slope[span[part], :] = early
            now[span[part], :] = start + 0.5 * TIME_STEP * (early + slopes[part])

    @pl.loop(0, rounds)
    def _(count):
        parity = count % 2
        stage = count % stages
        first = stage == 0
        moment = count // stages + jnp.minimum(stage, 1)

        @pl.loop(0, groups)
        def _(group):
            site_stage(group)

        @pl.loop(0, turns + CHIP_LAG)
        def _(turn):
            @pl.when(turn < turns)
            def _():
                for step in range(1, mom_size):
                    energy_copy(turn // pieces, turn % pieces, step).wait_recv()

                @pl.loop(0, chunk // 2)
                def _(couple):
                    for inner in range(2):
                        index = 2 * couple + inner
                        one_momentum((count * turns + turn) * chunk + index, turn, index)

                core_copy(parity, turn).start()

            @pl.when((turn >= CORE_LAG) & (turn < turns + CORE_LAG))
            def _():
                ready = turn - CORE_LAG
                core_copy(parity, ready).wait_recv()
                partial[ready, 1 - chip, core] = (
                    partial[ready, 1 - chip, core] + core_rows[parity, ready, 1 - chip]
                )
                chip_copy(parity, ready).start()

            @pl.when(turn >= CHIP_LAG)
            def _():
                ready = turn - CHIP_LAG
                chip_copy(parity, ready).wait_recv()

                @pl.loop(0, chunk)
                def _(inner):
                    update(parity, ready, inner, moment, first)

                @pl.when(count + 1 < rounds)
                def _():
                    publish(ready // pieces, ready % pieces)
                    send_rows(ready // pieces, ready % pieces)

                core_copy(parity, ready).wait_send()
                chip_copy(parity, ready).wait_send()

        @pl.loop(0, turns)
        def _(turn):
            for step in range(1, mom_size):
                energy_copy(turn // pieces, turn % pieces, step).wait_send()


def fits(mesh_sizes, new_rows):
    _, own_count, row_count, time_count = new_rows.shape
    return (
        mesh_sizes["tm"] == 4
        and mesh_sizes["mom"] % 8 == 0
        and row_count % mesh_sizes["mom"] == 0
        and own_count % 8 == 0
        and time_count % 128 == 0
    )


def advance(mom_size, new_rows, bands, mask_rows, tables, history):
    parts, own, rows, times = new_rows.shape
    full = history.shape[4]
    groups = rows // mom_size
    chunk = 8
    pieces = own // chunk
    turns = groups * pieces
    slots = min(16, own)
    lines = parts * mom_size
    vmem = pl.BlockSpec(memory_space=pltpu.VMEM)
    dma = pltpu.SemaphoreType.DMA
    f32 = jnp.float32
    flat = (parts * own * rows, times)
    result = pl.pallas_call(
        functools.partial(steps_kernel, mom_size, slots),
        out_shape=jax.ShapeDtypeStruct(flat, f32),
        in_specs=[vmem] * 7 + [pl.BlockSpec(memory_space=pl.ANY)],
        out_specs=vmem,
        scratch_shapes=[
            pltpu.VMEM(flat, f32),
            pltpu.VMEM(flat, f32),
            pltpu.VMEM((groups, mom_size, pieces, parts, chunk, times), f32),
            pltpu.VMEM((groups, mom_size, pieces, parts, chunk, times), f32),
            pltpu.VMEM((groups, mom_size, pieces, parts * chunk, times), f32),
            pltpu.VMEM((turns * mom_size * parts * chunk, times), f32),
            pltpu.VMEM((turns, 2, 2, chunk, lines, times), f32),
            pltpu.VMEM((2, turns, 2, chunk, lines, times), f32),
            pltpu.VMEM((2, turns, chunk, lines, times), f32),
            pltpu.VMEM((slots, 3, 2, times, full), f32),
            dma((slots,)),
            dma((groups, mom_size)),
            dma((groups, mom_size)),
            dma((groups, pieces, mom_size)),
            dma((groups, pieces, mom_size)),
            dma((turns,)),
            dma((2, turns)),
            dma((turns,)),
            dma((2, turns)),
        ],
        compiler_params=pltpu.CompilerParams(
            collective_id=0, has_side_effects=True, vmem_limit_bytes=60 * 1024 * 1024
        ),
        name="advance_rows",
    )(new_rows.reshape(flat), bands, mask_rows, *tables, history)
    return result.reshape(new_rows.shape)


def table_halves(table):
    high = lax.reduce_precision(table, exponent_bits=8, mantissa_bits=7)
    return high.astype(jnp.bfloat16), (table - high).astype(jnp.bfloat16)


def fused_body(mom_size, new_rows, history, momentum_map, step_index, history_len):
    own_count = new_rows.shape[1]
    row_count = new_rows.shape[2]
    time_count = new_rows.shape[3]
    cosine_table, sine_table = lattice_tables(momentum_map, SIDE)
    tables = table_halves(jnp.concatenate([cosine_table, sine_table], axis=0)) + table_halves(
        jnp.concatenate([cosine_table.T, sine_table.T], axis=0)
    )
    own_map = lax.dynamic_slice_in_dim(momentum_map, lax.axis_index("mom") * own_count, own_count, 0)
    positions = lax.axis_index("tm") * time_count + jnp.arange(time_count, dtype=jnp.int32)
    memory_mask = (positions < history_len[0]).astype(jnp.float32)
    mask_rows = jnp.broadcast_to(memory_mask[None, :], (8, time_count))
    first_times = step_index[0].astype(jnp.float32) + jnp.arange(row_count, dtype=jnp.int32).astype(
        jnp.float32
    )
    bands = jnp.stack(
        [
            band_energy(own_map, (first_times + float(offset)) * TIME_STEP, SIDE)
            for offset in range(STEPS + 1)
        ]
    )
    bands = jnp.broadcast_to(bands.reshape(-1, 1), (bands.size, time_count))
    return advance(mom_size, new_rows, bands, mask_rows, tables, history)


def solution(mesh):
    in_specs = (P(None, "mom", None, "tm"), P(None, None, "mom", "tm", None), P(), P(), P())
    out_specs = P(None, "mom", None, "tm")

    def dispatch(new_rows, *others):
        if fits(dict(mesh.shape), new_rows):
            return fused_body(mesh.shape["mom"], new_rows, *others)
        return body(new_rows, *others)

    return jax.shard_map(
        dispatch, mesh=mesh, in_specs=in_specs, out_specs=out_specs, check_vma=False
    )
```

```python
import functools

import jax
import jax.numpy as jnp
from jax import lax
from jax.experimental import pallas as pl
from jax.experimental.pallas import tpu as pltpu
from jax.sharding import PartitionSpec as P


SIDE = 16


TIME_STEP = 0.2
COUPLING = 5.0
DRIVE_RATE = 0.3
PRECISE = lax.Precision.HIGHEST


def lattice_tables(momentum_map, side):
    mom_count = momentum_map.shape[0]
    sites = jnp.arange(mom_count, dtype=jnp.int32)
    mom_x = momentum_map // side
    mom_y = momentum_map % side
    site_x = sites // side
    site_y = sites % side
    winding = (site_x[:, None] * mom_x[None, :] + site_y[:, None] * mom_y[None, :]) % side
    phases = winding.astype(jnp.float32) * (2.0 * jnp.pi / side)
    return (jnp.cos(phases), jnp.sin(phases))


def band_energy(own_map, row_times, side):
    wave_x = (own_map // side).astype(jnp.float32) * (2.0 * jnp.pi / side)
    wave_y = (own_map % side).astype(jnp.float32) * (2.0 * jnp.pi / side)
    drift = DRIVE_RATE * row_times
    return -2.0 * (
        jnp.cos(wave_x[:, None] + drift[None, :]) + jnp.cos(wave_y[:, None] + drift[None, :])
    )


def to_sites(cosine_table, sine_table, lattice):
    mom_count = lattice.shape[1]
    paired = lattice.reshape(2, 2, mom_count, lattice.shape[2])
    parts_re = paired[:, 0]
    parts_im = paired[:, 1]

    def apply_table(table, values):
        return jnp.einsum("rk,wkc->wrc", table, values, precision=PRECISE)

    site_re = (apply_table(cosine_table, parts_re) - apply_table(sine_table, parts_im)) / mom_count
    site_im = (apply_table(cosine_table, parts_im) + apply_table(sine_table, parts_re)) / mom_count
    return jnp.stack([site_re, site_im], axis=1).reshape(4, cosine_table.shape[0], lattice.shape[2])


def from_sites(cosine_table, sine_table, lattice):
    paired = lattice.reshape(2, 2, lattice.shape[1], lattice.shape[2])
    parts_re = paired[:, 0]
    parts_im = paired[:, 1]

    def apply_table(table, values):
        return jnp.einsum("rk,wrc->wkc", table, values, precision=PRECISE)

    mom_re = apply_table(cosine_table, parts_re) + apply_table(sine_table, parts_im)
    mom_im = apply_table(cosine_table, parts_im) - apply_table(sine_table, parts_re)
    return jnp.stack([mom_re, mom_im], axis=1).reshape(4, cosine_table.shape[1], lattice.shape[2])


def bubble_term(left_re, left_im, right_re, right_im):
    square_re = left_re * left_re - left_im * left_im
    square_im = 2.0 * left_re * left_im
    factor = -COUPLING * COUPLING
    return (
        factor * (square_re * right_re + square_im * right_im),
        factor * (square_im * right_re - square_re * right_im),
    )


def bubble(lattice):
    ret_re, ret_im, less_re, less_im = (lattice[0], lattice[1], lattice[2], lattice[3])
    great_re = less_re + ret_re
    great_im = less_im + ret_im
    lesser_re, lesser_im = bubble_term(less_re, less_im, great_re, great_im)
    greater_re, greater_im = bubble_term(great_re, great_im, less_re, less_im)
    return jnp.stack([greater_re - lesser_re, greater_im - lesser_im, lesser_re, lesser_im])


def contract(energy_pair, stored_pair):
    product = jnp.einsum("akiu,bkus->abkis", energy_pair, stored_pair, precision=PRECISE)
    return (product[0, 0] - product[1, 1], product[0, 1] + product[1, 0])


def memory_integral(self_energy, history):
    ret_ret = contract(self_energy[0:2], history[0])
    ret_less = contract(self_energy[0:2], history[1])
    less_adv = contract(self_energy[2:4], history[2])
    return TIME_STEP * jnp.stack(
        [ret_ret[0], ret_ret[1], ret_less[0] + less_adv[0], ret_less[1] + less_adv[1]]
    )


def rotate(total):
    return jnp.stack([total[1], -total[0], total[3], -total[2]])


def body(new_rows, history, momentum_map, step_index, history_len):
    own_count = new_rows.shape[1]
    row_count = new_rows.shape[2]
    time_count = new_rows.shape[3]
    cosine_table, sine_table = lattice_tables(momentum_map, SIDE)
    mom_start = lax.axis_index("mom") * own_count
    own_map = lax.dynamic_slice_in_dim(momentum_map, mom_start, own_count, 0)
    time_start = lax.axis_index("tm") * time_count
    positions = time_start + jnp.arange(time_count, dtype=jnp.int32)
    memory_mask = (positions < history_len[0]).astype(jnp.float32)
    first_times = step_index[0].astype(jnp.float32) + jnp.arange(row_count, dtype=jnp.int32).astype(
        jnp.float32
    )

    def slope(estimate, offset_steps):
        band = band_energy(own_map, (first_times + offset_steps) * TIME_STEP, SIDE)
        flattened = estimate.reshape(4, own_count, row_count * time_count)
        by_site = lax.all_to_all(flattened, "mom", split_axis=2, concat_axis=1, tiled=True)
        site_energy = from_sites(
            cosine_table, sine_table, bubble(to_sites(cosine_table, sine_table, by_site))
        )
        returned = lax.all_to_all(site_energy, "mom", split_axis=1, concat_axis=2, tiled=True)
        self_energy = returned.reshape(4, own_count, row_count, time_count)
        self_energy = self_energy * memory_mask
        partial_rows = memory_integral(self_energy, history)
        integral = lax.psum_scatter(partial_rows, "tm", scatter_dimension=3, tiled=True)
        return rotate(band[None, :, :, None] * estimate + integral)

    current = new_rows
    for time_step in range(2):
        slope_now = slope(current, float(time_step))
        estimate = current + TIME_STEP * slope_now
        for corrector in range(2):
            estimate = current + 0.5 * TIME_STEP * (
                slope_now + slope(estimate, float(time_step + 1))
            )
        current = estimate
    return current


MESH = pl.DeviceIdType.MESH


def halves(values):
    high = values.astype(jnp.bfloat16)
    return high, (values - high.astype(jnp.float32)).astype(jnp.bfloat16)


def product(left, right):
    return jnp.dot(left, right, preferred_element_type=jnp.float32)


def triple(left_high, left_low, right):
    right_high, right_low = halves(right)
    return (
        product(left_high, right_high)
        + product(left_high, right_low)
        + product(left_low, right_high)
    )


STEPS = 2
CORRECTORS = 2
CORE_LAG = 1
CHIP_LAG = 3
DEPTH = CHIP_LAG + 1
UNROLL = 4
RING = 4


def steps_kernel(
    mom_size,
    map_ref,
    step_ref,
    length_ref,
    state_ref,
    history_ref,
    now,
    base,
    first_slope,
    outgoing,
    gathered,
    energy,
    returned,
    partial,
    core_rows,
    chip_rows,
    stored,
    site_high,
    site_low,
    back_high,
    back_low,
    own_waves,
    time_waves,
    state_sem,
    stored_sem,
    row_send,
    row_recv,
    energy_send,
    energy_recv,
    core_send,
    core_recv,
    chip_send,
    chip_recv,
):
    mom = lax.axis_index("mom")
    tm = lax.axis_index("tm")
    core = tm % 2
    chip = tm // 2
    near = chip * 2 + (1 - core)
    far = (1 - chip) * 2 + core
    groups, _, pieces, _, chunk, times = outgoing.shape
    own = pieces * chunk
    rows = groups * mom_size
    sites = own * mom_size
    turns = groups * pieces
    stages = CORRECTORS + 1
    rounds = STEPS * stages
    quads = own // UNROLL
    resident = own - quads
    fetches = rounds * groups * quads

    def load(index, slot):
        return pltpu.make_async_copy(
            history_ref.at[:, :, index], stored.at[slot], stored_sem.at[slot]
        )

    def keep(quad, place):
        return load(quad * UNROLL + place, quad * (UNROLL - 1) + place)

    def fetch(count):
        return load(count % quads * UNROLL + UNROLL - 1, resident + count % RING)

    state_copy = pltpu.make_async_copy(state_ref, now, state_sem)
    state_copy.start()

    barrier = pltpu.get_barrier_semaphore()
    for step in range(1, mom_size):
        pl.semaphore_signal(
            barrier, inc=1, device_id={"mom": (mom + step) % mom_size}, device_id_type=MESH
        )
    for peer in (near, far):
        pl.semaphore_signal(barrier, inc=1, device_id={"tm": peer}, device_id_type=MESH)

    def peer_of(step):
        return (mom + step) % mom_size

    def row_copy(group, piece, step):
        return pltpu.make_async_remote_copy(
            src_ref=outgoing.at[group, peer_of(step), piece],
            dst_ref=gathered.at[group, mom, piece],
            send_sem=row_send.at[group, step],
            recv_sem=row_recv.at[group, step],
            device_id={"mom": peer_of(step)},
            device_id_type=MESH,
        )

    def all_rows(group, step):
        return pltpu.make_async_remote_copy(
            src_ref=outgoing.at[group, peer_of(step)],
            dst_ref=gathered.at[group, mom],
            send_sem=row_send.at[group, step],
            recv_sem=row_recv.at[group, step],
            device_id={"mom": peer_of(step)},
            device_id_type=MESH,
        )

    def landing(group, piece):
        depth = 4 * chunk
        start = ((group * pieces + piece) * mom_size + mom) * depth
        return pl.ds(pl.multiple_of(start, depth), depth)

    def energy_copy(group, piece, step):
        return pltpu.make_async_remote_copy(
            src_ref=energy.at[group, peer_of(step), piece],
            dst_ref=returned.at[landing(group, piece)],
            send_sem=energy_send.at[group, piece, step],
            recv_sem=energy_recv.at[group, piece, step],
            device_id={"mom": peer_of(step)},
            device_id_type=MESH,
        )

    def core_copy(turn):
        return pltpu.make_async_remote_copy(
            src_ref=partial.at[turn % DEPTH, :, 1 - core],
            dst_ref=core_rows.at[turn],
            send_sem=core_send.at[turn],
            recv_sem=core_recv.at[turn],
            device_id={"tm": near},
            device_id_type=MESH,
        )

    def chip_copy(turn):
        return pltpu.make_async_remote_copy(
            src_ref=partial.at[turn % DEPTH, 1 - chip, core],
            dst_ref=chip_rows.at[turn],
            send_sem=chip_send.at[turn],
            recv_sem=chip_recv.at[turn],
            device_id={"tm": far},
            device_id_type=MESH,
        )

    def publish(group, piece):
        for part in range(4):
            for row in range(mom_size):
                start = (part * own + piece * chunk) * rows + group * mom_size + row
                outgoing[group, row, piece, part] = now[pl.ds(start, chunk, stride=rows), :]
        gathered[group, mom, piece] = outgoing[group, mom, piece]

    def send_rows(group, piece):
        for step in range(1, mom_size):
            row_copy(group, piece, step).start()

    state_copy.wait()
    pl.semaphore_wait(barrier, mom_size + 1)

    @pl.loop(0, turns)
    def _(turn):
        publish(turn // pieces, turn % pieces)
        send_rows(turn // pieces, turn % pieces)

    @pl.loop(0, quads)
    def _(quad):
        for place in range(UNROLL - 1):
            keep(quad, place).start()

        @pl.when(quad < RING)
        def _():
            fetch(quad).start()

    square = (sites, sites)
    turn_of = 2.0 * jnp.pi / SIDE
    place_row = jnp.broadcast_to(map_ref[0:1, :], square)
    place_column = jnp.transpose(place_row.astype(jnp.float32)).astype(jnp.int32)

    def table_of(first, second, high_ref, low_ref):
        winding = (first // SIDE) * (second // SIDE) + (first % SIDE) * (second % SIDE)
        phases = (winding % SIDE).astype(jnp.float32) * turn_of
        for half, values in enumerate((jnp.cos(phases), jnp.sin(phases))):
            high, low = halves(values)
            high_ref[half * sites : (half + 1) * sites] = high
            low_ref[half * sites : (half + 1) * sites] = low

    table_of(lax.broadcasted_iota(jnp.int32, square, 0), place_row, site_high, site_low)
    table_of(place_column, lax.broadcasted_iota(jnp.int32, square, 1), back_high, back_low)

    column = place_column[:, :times]
    for kind, index in enumerate((column // SIDE, column % SIDE)):
        wave = index.astype(jnp.float32) * turn_of
        own_waves[2 * kind] = jnp.cos(wave)
        own_waves[2 * kind + 1] = jnp.sin(wave)
    late = (STEPS + 1) * rows
    label = lax.broadcasted_iota(jnp.int32, (late, times), 0)
    ahead = label % rows + label // rows
    drift = DRIVE_RATE * ((step_ref[0] + ahead).astype(jnp.float32) * TIME_STEP)
    time_waves[0] = jnp.cos(drift)
    time_waves[1] = jnp.sin(drift)
    position = tm * times + lax.broadcasted_iota(jnp.int32, (1, times), 1)
    mask = (position < length_ref[0]).astype(jnp.float32)

    def site_stage(group):
        for step in range(1, mom_size):
            all_rows(group, step).wait_recv()
        fields = []
        for pair in range(2):
            both = jnp.concatenate(
                [gathered[group, :, :, 2 * pair + part].reshape(sites, times) for part in range(2)],
                axis=1,
            )
            turned = triple(site_high[...], site_low[...], both)
            fields.append((turned[:sites, :times] - turned[sites:, times:]) / sites)
            fields.append((turned[:sites, times:] + turned[sites:, :times]) / sites)
        ret_re, ret_im, less_re, less_im = fields
        great_re = less_re + ret_re
        great_im = less_im + ret_im
        lesser_re, lesser_im = bubble_term(less_re, less_im, great_re, great_im)
        greater_re, greater_im = bubble_term(great_re, great_im, less_re, less_im)
        pairs = (
            (greater_re - lesser_re, greater_im - lesser_im),
            (lesser_re, lesser_im),
        )
        for pair, (part_re, part_im) in enumerate(pairs):
            both = jnp.concatenate([part_re, part_im], axis=1)
            turned = triple(back_high[...], back_low[...], both)
            mom_re = (turned[:sites, :times] + turned[sites:, times:]) * mask
            mom_im = (turned[:sites, times:] - turned[sites:, :times]) * mask
            for part, values in ((2 * pair, mom_re), (2 * pair + 1, mom_im)):
                window = pl.ds(part * chunk, chunk)
                energy[group, :, :, window] = values.reshape(mom_size, pieces, chunk, times)

        @pl.loop(0, pieces)
        def _(piece):
            for step in range(1, mom_size):
                energy_copy(group, piece, step).start()
            returned[landing(group, piece)] = energy[group, mom, piece]

        for step in range(1, mom_size):
            all_rows(group, step).wait_send()

    def one_momentum(slot, turn, inner):
        depth = 4 * chunk
        start = turn * mom_size * depth + inner
        ret_re, ret_im, less_re, less_im = [
            returned[pl.ds(start + part * chunk, mom_size, stride=depth), :] for part in range(4)
        ]
        lines = 2 * mom_size

        def folded(part_re, part_im):
            return jnp.concatenate(
                [
                    jnp.concatenate([part_re, -part_im], axis=1),
                    jnp.concatenate([part_im, part_re], axis=1),
                ],
                axis=0,
            )

        def applied(high, both, kind):
            weights_high, weights_low = halves(stored[slot, kind].reshape(2 * times, -1))
            stacked = product(both, weights_high)
            return stacked[:lines] + stacked[lines:] + product(high, weights_low)

        ret_high, ret_low = halves(folded(ret_re, ret_im))
        ret_both = jnp.concatenate([ret_high, ret_low], axis=0)
        less_high, less_low = halves(folded(less_re, less_im))
        less_both = jnp.concatenate([less_high, less_low], axis=0)
        ret_sum = applied(ret_high, ret_both, 0)
        less_sum = applied(ret_high, ret_both, 1) + applied(less_high, less_both, 2)
        for block in range(4):
            window = slice(block * times, (block + 1) * times)
            partial[turn % DEPTH, block // 2, block % 2, inner, :lines] = ret_sum[:, window]
            partial[turn % DEPTH, block // 2, block % 2, inner, lines:] = less_sum[:, window]

    def update(turn, inner, moment, first):
        group = turn // pieces
        index = (turn % pieces) * chunk + inner
        total = (
            partial[turn % DEPTH, chip, core, inner]
            + core_rows[turn, chip, inner]
            + chip_rows[turn, inner]
        )
        span = [
            pl.ds(
                pl.multiple_of((part * own + index) * rows + group * mom_size, mom_size), mom_size
            )
            for part in range(4)
        ]
        instant = pl.ds(pl.multiple_of(moment * rows + group * mom_size, mom_size), mom_size)
        wave = [own_waves[kind, pl.ds(mom * own + index, 1), :] for kind in range(4)]
        band = -2.0 * (
            (wave[0] + wave[2]) * time_waves[0, instant]
            - (wave[1] + wave[3]) * time_waves[1, instant]
        )
        terms = [
            band * now[span[part], :] + TIME_STEP * total[part * mom_size : (part + 1) * mom_size]
            for part in range(4)
        ]
        slopes = (terms[1], -terms[0], terms[3], -terms[2])
        for part in range(4):
            start = jnp.where(first, now[span[part], :], base[span[part], :])
            early = jnp.where(first, slopes[part], first_slope[span[part], :])
            base[span[part], :] = start
            first_slope[span[part], :] = early
            now[span[part], :] = start + 0.5 * TIME_STEP * (early + slopes[part])

    @pl.loop(0, rounds)
    def _(count):
        stage = count % stages
        first = stage == 0
        moment = count // stages + jnp.minimum(stage, 1)

        @pl.loop(0, groups)
        def _(group):
            site_stage(group)

        @pl.loop(0, turns + CHIP_LAG)
        def _(turn):
            @pl.when(turn < turns)
            def _():
                for step in range(1, mom_size):
                    energy_copy(turn // pieces, turn % pieces, step).wait_recv()

                @pl.loop(0, chunk // UNROLL)
                def _(part):
                    quad = turn % pieces * (chunk // UNROLL) + part
                    serial = (count * turns + turn) * (chunk // UNROLL) + part

                    @pl.when((count == 0) & (turn < pieces))
                    def _():
                        for place in range(UNROLL - 1):
                            keep(quad, place).wait()

                    fetch(serial).wait()
                    for place in range(UNROLL - 1):
                        one_momentum(
                            quad * (UNROLL - 1) + place, turn, part * UNROLL + place
                        )
                    one_momentum(
                        resident + serial % RING, turn, part * UNROLL + UNROLL - 1
                    )

                    @pl.when(serial + RING < fetches)
                    def _():
                        fetch(serial + RING).start()

                core_copy(turn).start()

            @pl.when((turn >= CORE_LAG) & (turn < turns + CORE_LAG))
            def _():
                ready = turn - CORE_LAG
                core_copy(ready).wait_recv()
                partial[ready % DEPTH, 1 - chip, core] = (
                    partial[ready % DEPTH, 1 - chip, core] + core_rows[ready, 1 - chip]
                )
                chip_copy(ready).start()

            @pl.when(turn >= CHIP_LAG)
            def _():
                ready = turn - CHIP_LAG
                chip_copy(ready).wait_recv()

                @pl.loop(0, chunk)
                def _(inner):
                    update(ready, inner, moment, first)

                @pl.when(count + 1 < rounds)
                def _():
                    publish(ready // pieces, ready % pieces)
                    send_rows(ready // pieces, ready % pieces)

                core_copy(ready).wait_send()
                chip_copy(ready).wait_send()

        @pl.loop(0, turns)
        def _(turn):
            for step in range(1, mom_size):
                energy_copy(turn // pieces, turn % pieces, step).wait_send()


def fits(mesh_sizes, new_rows):
    _, own_count, row_count, time_count = new_rows.shape
    return (
        mesh_sizes["tm"] == 4
        and mesh_sizes["mom"] % 8 == 0
        and row_count % mesh_sizes["mom"] == 0
        and row_count * own_count >= 64 * mesh_sizes["mom"]
        and own_count % 8 == 0
        and time_count % 128 == 0
        and time_count <= own_count * mesh_sizes["mom"]
    )


def advance(mom_size, new_rows, history, momentum_map, step_index, history_len):
    parts, own, rows, times = new_rows.shape
    full = history.shape[4]
    groups = rows // mom_size
    chunk = 8
    pieces = own // chunk
    turns = groups * pieces
    slots = own - own // UNROLL + RING
    lines = parts * mom_size
    sites = own * mom_size
    vmem = pl.BlockSpec(memory_space=pltpu.VMEM)
    smem = pl.BlockSpec(memory_space=pltpu.SMEM)
    whole = pl.BlockSpec(memory_space=pl.ANY)
    table = pltpu.VMEM((2 * sites, sites), jnp.bfloat16)
    dma = pltpu.SemaphoreType.DMA
    f32 = jnp.float32
    flat = (parts * own * rows, times)
    result = pl.pallas_call(
        functools.partial(steps_kernel, mom_size),
        out_shape=jax.ShapeDtypeStruct(flat, f32),
        in_specs=[vmem, smem, smem, whole, whole],
        out_specs=vmem,
        scratch_shapes=[
            pltpu.VMEM(flat, f32),
            pltpu.VMEM(flat, f32),
            pltpu.VMEM((groups, mom_size, pieces, parts, chunk, times), f32),
            pltpu.VMEM((groups, mom_size, pieces, parts, chunk, times), f32),
            pltpu.VMEM((groups, mom_size, pieces, parts * chunk, times), f32),
            pltpu.VMEM((turns * mom_size * parts * chunk, times), f32),
            pltpu.VMEM((DEPTH, 2, 2, chunk, lines, times), f32),
            pltpu.VMEM((turns, 2, chunk, lines, times), f32),
            pltpu.VMEM((turns, chunk, lines, times), f32),
            pltpu.VMEM((slots, 3, 2, times, full), f32),
            table,
            table,
            table,
            table,
            pltpu.VMEM((4, sites, times), f32),
            pltpu.VMEM((2, (STEPS + 1) * rows, times), f32),
            dma(()),
            dma((slots,)),
            dma((groups, mom_size)),
            dma((groups, mom_size)),
            dma((groups, pieces, mom_size)),
            dma((groups, pieces, mom_size)),
            dma((turns,)),
            dma((turns,)),
            dma((turns,)),
            dma((turns,)),
        ],
        compiler_params=pltpu.CompilerParams(
            collective_id=0, has_side_effects=True, vmem_limit_bytes=63 * 1024 * 1024
        ),
        name="advance_rows",
    )(momentum_map.reshape(1, -1), step_index, history_len, new_rows.reshape(flat), history)
    return result.reshape(new_rows.shape)


def solution(mesh):
    in_specs = (P(None, "mom", None, "tm"), P(None, None, "mom", "tm", None), P(), P(), P())
    out_specs = P(None, "mom", None, "tm")

    def dispatch(new_rows, *others):
        if fits(dict(mesh.shape), new_rows):
            return advance(mesh.shape["mom"], new_rows, *others)
        return body(new_rows, *others)

    return jax.shard_map(
        dispatch, mesh=mesh, in_specs=in_specs, out_specs=out_specs, check_vma=False
    )
```

```python
import functools

import jax
import jax.numpy as jnp
from jax import lax
from jax.experimental import pallas as pl
from jax.experimental.pallas import tpu as pltpu
from jax.sharding import PartitionSpec as P


SIDE = 16


TIME_STEP = 0.2
COUPLING = 5.0
DRIVE_RATE = 0.3
PRECISE = lax.Precision.HIGHEST


def lattice_tables(momentum_map, side):
    mom_count = momentum_map.shape[0]
    sites = jnp.arange(mom_count, dtype=jnp.int32)
    mom_x = momentum_map // side
    mom_y = momentum_map % side
    site_x = sites // side
    site_y = sites % side
    winding = (site_x[:, None] * mom_x[None, :] + site_y[:, None] * mom_y[None, :]) % side
    phases = winding.astype(jnp.float32) * (2.0 * jnp.pi / side)
    return (jnp.cos(phases), jnp.sin(phases))


def band_energy(own_map, row_times, side):
    wave_x = (own_map // side).astype(jnp.float32) * (2.0 * jnp.pi / side)
    wave_y = (own_map % side).astype(jnp.float32) * (2.0 * jnp.pi / side)
    drift = DRIVE_RATE * row_times
    return -2.0 * (
        jnp.cos(wave_x[:, None] + drift[None, :]) + jnp.cos(wave_y[:, None] + drift[None, :])
    )


def to_sites(cosine_table, sine_table, lattice):
    mom_count = lattice.shape[1]
    paired = lattice.reshape(2, 2, mom_count, lattice.shape[2])
    parts_re = paired[:, 0]
    parts_im = paired[:, 1]

    def apply_table(table, values):
        return jnp.einsum("rk,wkc->wrc", table, values, precision=PRECISE)

    site_re = (apply_table(cosine_table, parts_re) - apply_table(sine_table, parts_im)) / mom_count
    site_im = (apply_table(cosine_table, parts_im) + apply_table(sine_table, parts_re)) / mom_count
    return jnp.stack([site_re, site_im], axis=1).reshape(4, cosine_table.shape[0], lattice.shape[2])


def from_sites(cosine_table, sine_table, lattice):
    paired = lattice.reshape(2, 2, lattice.shape[1], lattice.shape[2])
    parts_re = paired[:, 0]
    parts_im = paired[:, 1]

    def apply_table(table, values):
        return jnp.einsum("rk,wrc->wkc", table, values, precision=PRECISE)

    mom_re = apply_table(cosine_table, parts_re) + apply_table(sine_table, parts_im)
    mom_im = apply_table(cosine_table, parts_im) - apply_table(sine_table, parts_re)
    return jnp.stack([mom_re, mom_im], axis=1).reshape(4, cosine_table.shape[1], lattice.shape[2])


def bubble_term(left_re, left_im, right_re, right_im):
    square_re = left_re * left_re - left_im * left_im
    square_im = 2.0 * left_re * left_im
    factor = -COUPLING * COUPLING
    return (
        factor * (square_re * right_re + square_im * right_im),
        factor * (square_im * right_re - square_re * right_im),
    )


def bubble(lattice):
    ret_re, ret_im, less_re, less_im = (lattice[0], lattice[1], lattice[2], lattice[3])
    great_re = less_re + ret_re
    great_im = less_im + ret_im
    lesser_re, lesser_im = bubble_term(less_re, less_im, great_re, great_im)
    greater_re, greater_im = bubble_term(great_re, great_im, less_re, less_im)
    return jnp.stack([greater_re - lesser_re, greater_im - lesser_im, lesser_re, lesser_im])


def contract(energy_pair, stored_pair):
    product = jnp.einsum("akiu,bkus->abkis", energy_pair, stored_pair, precision=PRECISE)
    return (product[0, 0] - product[1, 1], product[0, 1] + product[1, 0])


def memory_integral(self_energy, history):
    ret_ret = contract(self_energy[0:2], history[0])
    ret_less = contract(self_energy[0:2], history[1])
    less_adv = contract(self_energy[2:4], history[2])
    return TIME_STEP * jnp.stack(
        [ret_ret[0], ret_ret[1], ret_less[0] + less_adv[0], ret_less[1] + less_adv[1]]
    )


def rotate(total):
    return jnp.stack([total[1], -total[0], total[3], -total[2]])


def body(new_rows, history, momentum_map, step_index, history_len):
    own_count = new_rows.shape[1]
    row_count = new_rows.shape[2]
    time_count = new_rows.shape[3]
    cosine_table, sine_table = lattice_tables(momentum_map, SIDE)
    mom_start = lax.axis_index("mom") * own_count
    own_map = lax.dynamic_slice_in_dim(momentum_map, mom_start, own_count, 0)
    time_start = lax.axis_index("tm") * time_count
    positions = time_start + jnp.arange(time_count, dtype=jnp.int32)
    memory_mask = (positions < history_len[0]).astype(jnp.float32)
    first_times = step_index[0].astype(jnp.float32) + jnp.arange(row_count, dtype=jnp.int32).astype(
        jnp.float32
    )

    def slope(estimate, offset_steps):
        band = band_energy(own_map, (first_times + offset_steps) * TIME_STEP, SIDE)
        flattened = estimate.reshape(4, own_count, row_count * time_count)
        by_site = lax.all_to_all(flattened, "mom", split_axis=2, concat_axis=1, tiled=True)
        site_energy = from_sites(
            cosine_table, sine_table, bubble(to_sites(cosine_table, sine_table, by_site))
        )
        returned = lax.all_to_all(site_energy, "mom", split_axis=1, concat_axis=2, tiled=True)
        self_energy = returned.reshape(4, own_count, row_count, time_count)
        self_energy = self_energy * memory_mask
        partial_rows = memory_integral(self_energy, history)
        integral = lax.psum_scatter(partial_rows, "tm", scatter_dimension=3, tiled=True)
        return rotate(band[None, :, :, None] * estimate + integral)

    current = new_rows
    for time_step in range(2):
        slope_now = slope(current, float(time_step))
        estimate = current + TIME_STEP * slope_now
        for corrector in range(2):
            estimate = current + 0.5 * TIME_STEP * (
                slope_now + slope(estimate, float(time_step + 1))
            )
        current = estimate
    return current


MESH = pl.DeviceIdType.MESH


def halves(values):
    high = values.astype(jnp.bfloat16)
    return high, (values - high.astype(jnp.float32)).astype(jnp.bfloat16)


def product(left, right):
    return jnp.dot(left, right, preferred_element_type=jnp.float32)


def triple(left_high, left_low, right):
    right_high, right_low = halves(right)
    return (
        product(left_high, right_high)
        + product(left_high, right_low)
        + product(left_low, right_high)
    )


STEPS = 2
CORRECTORS = 2
CORE_LAG = 2
CHIP_LAG = 5
DEPTH = CHIP_LAG + 1
UNROLL = 4
RING = 4


def steps_kernel(
    mom_size,
    map_ref,
    step_ref,
    length_ref,
    state_ref,
    history_ref,
    now,
    base,
    first_slope,
    outgoing,
    gathered,
    energy,
    returned,
    partial,
    core_rows,
    chip_rows,
    stored,
    site_high,
    site_low,
    back_high,
    back_low,
    own_waves,
    time_waves,
    state_sem,
    stored_sem,
    row_send,
    row_recv,
    energy_send,
    energy_recv,
    core_send,
    core_recv,
    chip_send,
    chip_recv,
):
    mom = lax.axis_index("mom")
    tm = lax.axis_index("tm")
    core = tm % 2
    chip = tm // 2
    near = chip * 2 + (1 - core)
    far = (1 - chip) * 2 + core
    groups, _, pieces, _, chunk, times = outgoing.shape
    own = pieces * chunk
    rows = groups * mom_size
    sites = own * mom_size
    turns = groups * pieces
    stages = CORRECTORS + 1
    rounds = STEPS * stages
    quads = own // UNROLL
    resident = own - quads
    units = groups * quads
    halves_of = quads // pieces
    fetches = rounds * units

    def load(index, slot):
        return pltpu.make_async_copy(
            history_ref.at[:, :, index], stored.at[slot], stored_sem.at[slot]
        )

    def keep(quad, place):
        return load(quad * UNROLL + place, quad * (UNROLL - 1) + place)

    def fetch(count):
        return load(count % quads * UNROLL + UNROLL - 1, resident + count % RING)

    state_copy = pltpu.make_async_copy(state_ref, now, state_sem)
    state_copy.start()

    barrier = pltpu.get_barrier_semaphore()
    for step in range(1, mom_size):
        pl.semaphore_signal(
            barrier, inc=1, device_id={"mom": (mom + step) % mom_size}, device_id_type=MESH
        )
    for peer in (near, far):
        pl.semaphore_signal(barrier, inc=1, device_id={"tm": peer}, device_id_type=MESH)

    def peer_of(step):
        return (mom + step) % mom_size

    def row_copy(group, piece, step):
        return pltpu.make_async_remote_copy(
            src_ref=outgoing.at[group, peer_of(step), piece],
            dst_ref=gathered.at[group, mom, piece],
            send_sem=row_send.at[group, step],
            recv_sem=row_recv.at[group, step],
            device_id={"mom": peer_of(step)},
            device_id_type=MESH,
        )

    def all_rows(group, step):
        return pltpu.make_async_remote_copy(
            src_ref=outgoing.at[group, peer_of(step)],
            dst_ref=gathered.at[group, mom],
            send_sem=row_send.at[group, step],
            recv_sem=row_recv.at[group, step],
            device_id={"mom": peer_of(step)},
            device_id_type=MESH,
        )

    def landing(group, piece):
        depth = 4 * chunk
        start = ((group * pieces + piece) * mom_size + mom) * depth
        return pl.ds(pl.multiple_of(start, depth), depth)

    def energy_copy(group, piece, step):
        return pltpu.make_async_remote_copy(
            src_ref=energy.at[group, peer_of(step), piece],
            dst_ref=returned.at[landing(group, piece)],
            send_sem=energy_send.at[group, piece, step],
            recv_sem=energy_recv.at[group, piece, step],
            device_id={"mom": peer_of(step)},
            device_id_type=MESH,
        )

    def core_copy(unit):
        return pltpu.make_async_remote_copy(
            src_ref=partial.at[unit % DEPTH, :, 1 - core],
            dst_ref=core_rows.at[unit],
            send_sem=core_send.at[unit],
            recv_sem=core_recv.at[unit],
            device_id={"tm": near},
            device_id_type=MESH,
        )

    def chip_copy(unit):
        return pltpu.make_async_remote_copy(
            src_ref=partial.at[unit % DEPTH, 1 - chip, core],
            dst_ref=chip_rows.at[unit],
            send_sem=chip_send.at[unit],
            recv_sem=chip_recv.at[unit],
            device_id={"tm": far},
            device_id_type=MESH,
        )

    def publish(group, piece):
        for part in range(4):
            for row in range(mom_size):
                start = (part * own + piece * chunk) * rows + group * mom_size + row
                outgoing[group, row, piece, part] = now[pl.ds(start, chunk, stride=rows), :]
        gathered[group, mom, piece] = outgoing[group, mom, piece]

    def send_rows(group, piece):
        for step in range(1, mom_size):
            row_copy(group, piece, step).start()

    state_copy.wait()
    pl.semaphore_wait(barrier, mom_size + 1)

    @pl.loop(0, turns)
    def _(turn):
        publish(turn // pieces, turn % pieces)
        send_rows(turn // pieces, turn % pieces)

    @pl.loop(0, quads)
    def _(quad):
        for place in range(UNROLL - 1):
            keep(quad, place).start()

        @pl.when(quad < RING)
        def _():
            fetch(quad).start()

    square = (sites, sites)
    turn_of = 2.0 * jnp.pi / SIDE
    place_row = jnp.broadcast_to(map_ref[0:1, :], square)
    place_column = jnp.transpose(place_row.astype(jnp.float32)).astype(jnp.int32)

    def table_of(first, second, high_ref, low_ref):
        winding = (first // SIDE) * (second // SIDE) + (first % SIDE) * (second % SIDE)
        phases = (winding % SIDE).astype(jnp.float32) * turn_of
        for half, values in enumerate((jnp.cos(phases), jnp.sin(phases))):
            high, low = halves(values)
            high_ref[half * sites : (half + 1) * sites] = high
            low_ref[half * sites : (half + 1) * sites] = low

    table_of(lax.broadcasted_iota(jnp.int32, square, 0), place_row, site_high, site_low)
    table_of(place_column, lax.broadcasted_iota(jnp.int32, square, 1), back_high, back_low)

    column = place_column[:, :times]
    for kind, index in enumerate((column // SIDE, column % SIDE)):
        wave = index.astype(jnp.float32) * turn_of
        own_waves[2 * kind] = jnp.cos(wave)
        own_waves[2 * kind + 1] = jnp.sin(wave)
    late = (STEPS + 1) * rows
    label = lax.broadcasted_iota(jnp.int32, (late, times), 0)
    ahead = label % rows + label // rows
    drift = DRIVE_RATE * ((step_ref[0] + ahead).astype(jnp.float32) * TIME_STEP)
    time_waves[0] = jnp.cos(drift)
    time_waves[1] = jnp.sin(drift)
    position = tm * times + lax.broadcasted_iota(jnp.int32, (1, times), 1)
    mask = (position < length_ref[0]).astype(jnp.float32)

    def site_stage(group):
        for step in range(1, mom_size):
            all_rows(group, step).wait_recv()
        fields = []
        for pair in range(2):
            both = jnp.concatenate(
                [gathered[group, :, :, 2 * pair + part].reshape(sites, times) for part in range(2)],
                axis=1,
            )
            turned = triple(site_high[...], site_low[...], both)
            fields.append((turned[:sites, :times] - turned[sites:, times:]) / sites)
            fields.append((turned[:sites, times:] + turned[sites:, :times]) / sites)
        ret_re, ret_im, less_re, less_im = fields
        great_re = less_re + ret_re
        great_im = less_im + ret_im
        lesser_re, lesser_im = bubble_term(less_re, less_im, great_re, great_im)
        greater_re, greater_im = bubble_term(great_re, great_im, less_re, less_im)
        pairs = (
            (greater_re - lesser_re, greater_im - lesser_im),
            (lesser_re, lesser_im),
        )
        for pair, (part_re, part_im) in enumerate(pairs):
            both = jnp.concatenate([part_re, part_im], axis=1)
            turned = triple(back_high[...], back_low[...], both)
            mom_re = (turned[:sites, :times] + turned[sites:, times:]) * mask
            mom_im = (turned[:sites, times:] - turned[sites:, :times]) * mask
            for part, values in ((2 * pair, mom_re), (2 * pair + 1, mom_im)):
                window = pl.ds(part * chunk, chunk)
                energy[group, :, :, window] = values.reshape(mom_size, pieces, chunk, times)

        @pl.loop(0, pieces)
        def _(piece):
            for step in range(1, mom_size):
                energy_copy(group, piece, step).start()
            returned[landing(group, piece)] = energy[group, mom, piece]

        for step in range(1, mom_size):
            all_rows(group, step).wait_send()

    def one_momentum(slot, unit, place):
        depth = 4 * chunk
        start = unit // halves_of * mom_size * depth + unit % halves_of * UNROLL + place
        ret_re, ret_im, less_re, less_im = [
            returned[pl.ds(start + part * chunk, mom_size, stride=depth), :] for part in range(4)
        ]
        lines = 2 * mom_size

        def folded(part_re, part_im):
            return jnp.concatenate(
                [
                    jnp.concatenate([part_re, -part_im], axis=1),
                    jnp.concatenate([part_im, part_re], axis=1),
                ],
                axis=0,
            )

        def applied(high, both, kind):
            weights_high, weights_low = halves(stored[slot, kind].reshape(2 * times, -1))
            stacked = product(both, weights_high)
            return stacked[:lines] + stacked[lines:] + product(high, weights_low)

        ret_high, ret_low = halves(folded(ret_re, ret_im))
        ret_both = jnp.concatenate([ret_high, ret_low], axis=0)
        less_high, less_low = halves(folded(less_re, less_im))
        less_both = jnp.concatenate([less_high, less_low], axis=0)
        ret_sum = applied(ret_high, ret_both, 0)
        less_sum = applied(ret_high, ret_both, 1) + applied(less_high, less_both, 2)
        for block in range(4):
            window = slice(block * times, (block + 1) * times)
            partial[unit % DEPTH, block // 2, block % 2, place, :lines] = ret_sum[:, window]
            partial[unit % DEPTH, block // 2, block % 2, place, lines:] = less_sum[:, window]

    def update(unit, place, moment, first):
        group = unit // quads
        index = unit % quads * UNROLL + place
        total = (
            partial[unit % DEPTH, chip, core, place]
            + core_rows[unit, chip, place]
            + chip_rows[unit, place]
        )
        span = [
            pl.ds(
                pl.multiple_of((part * own + index) * rows + group * mom_size, mom_size), mom_size
            )
            for part in range(4)
        ]
        instant = pl.ds(pl.multiple_of(moment * rows + group * mom_size, mom_size), mom_size)
        wave = [own_waves[kind, pl.ds(mom * own + index, 1), :] for kind in range(4)]
        band = -2.0 * (
            (wave[0] + wave[2]) * time_waves[0, instant]
            - (wave[1] + wave[3]) * time_waves[1, instant]
        )
        terms = [
            band * now[span[part], :] + TIME_STEP * total[part * mom_size : (part + 1) * mom_size]
            for part in range(4)
        ]
        slopes = (terms[1], -terms[0], terms[3], -terms[2])
        for part in range(4):
            start = jnp.where(first, now[span[part], :], base[span[part], :])
            early = jnp.where(first, slopes[part], first_slope[span[part], :])
            base[span[part], :] = start
            first_slope[span[part], :] = early
            now[span[part], :] = start + 0.5 * TIME_STEP * (early + slopes[part])

    @pl.loop(0, rounds)
    def _(count):
        stage = count % stages
        first = stage == 0
        moment = count // stages + jnp.minimum(stage, 1)

        @pl.loop(0, groups)
        def _(group):
            site_stage(group)

        @pl.loop(0, units + CHIP_LAG)
        def _(unit):
            @pl.when(unit < units)
            def _():
                turn = unit // halves_of
                quad = unit % quads
                serial = count * units + unit

                @pl.when(unit % halves_of == 0)
                def _():
                    for step in range(1, mom_size):
                        energy_copy(turn // pieces, turn % pieces, step).wait_recv()

                @pl.when((count == 0) & (unit < quads))
                def _():
                    for place in range(UNROLL - 1):
                        keep(quad, place).wait()

                fetch(serial).wait()
                for place in range(UNROLL - 1):
                    one_momentum(quad * (UNROLL - 1) + place, unit, place)
                one_momentum(resident + serial % RING, unit, UNROLL - 1)

                @pl.when(serial + RING < fetches)
                def _():
                    fetch(serial + RING).start()

                core_copy(unit).start()

            @pl.when((unit >= CORE_LAG) & (unit < units + CORE_LAG))
            def _():
                ready = unit - CORE_LAG
                core_copy(ready).wait_recv()
                partial[ready % DEPTH, 1 - chip, core] = (
                    partial[ready % DEPTH, 1 - chip, core] + core_rows[ready, 1 - chip]
                )
                chip_copy(ready).start()

            @pl.when(unit >= CHIP_LAG)
            def _():
                ready = unit - CHIP_LAG
                chip_copy(ready).wait_recv()

                @pl.loop(0, UNROLL)
                def _(place):
                    update(ready, place, moment, first)

                @pl.when((count + 1 < rounds) & (ready % halves_of == halves_of - 1))
                def _():
                    turn = ready // halves_of
                    publish(turn // pieces, turn % pieces)
                    send_rows(turn // pieces, turn % pieces)

                core_copy(ready).wait_send()
                chip_copy(ready).wait_send()

        @pl.loop(0, turns)
        def _(turn):
            for step in range(1, mom_size):
                energy_copy(turn // pieces, turn % pieces, step).wait_send()


def fits(mesh_sizes, new_rows):
    _, own_count, row_count, time_count = new_rows.shape
    return (
        mesh_sizes["tm"] == 4
        and mesh_sizes["mom"] % 8 == 0
        and row_count % mesh_sizes["mom"] == 0
        and row_count * own_count >= 64 * mesh_sizes["mom"]
        and own_count % 8 == 0
        and time_count % 128 == 0
        and time_count <= own_count * mesh_sizes["mom"]
    )


def advance(mom_size, new_rows, history, momentum_map, step_index, history_len):
    parts, own, rows, times = new_rows.shape
    full = history.shape[4]
    groups = rows // mom_size
    chunk = 8
    pieces = own // chunk
    turns = groups * pieces
    units = groups * (own // UNROLL)
    slots = own - own // UNROLL + RING
    lines = parts * mom_size
    sites = own * mom_size
    vmem = pl.BlockSpec(memory_space=pltpu.VMEM)
    smem = pl.BlockSpec(memory_space=pltpu.SMEM)
    whole = pl.BlockSpec(memory_space=pl.ANY)
    table = pltpu.VMEM((2 * sites, sites), jnp.bfloat16)
    dma = pltpu.SemaphoreType.DMA
    f32 = jnp.float32
    flat = (parts * own * rows, times)
    result = pl.pallas_call(
        functools.partial(steps_kernel, mom_size),
        out_shape=jax.ShapeDtypeStruct(flat, f32),
        in_specs=[vmem, smem, smem, whole, whole],
        out_specs=vmem,
        scratch_shapes=[
            pltpu.VMEM(flat, f32),
            pltpu.VMEM(flat, f32),
            pltpu.VMEM((groups, mom_size, pieces, parts, chunk, times), f32),
            pltpu.VMEM((groups, mom_size, pieces, parts, chunk, times), f32),
            pltpu.VMEM((groups, mom_size, pieces, parts * chunk, times), f32),
            pltpu.VMEM((turns * mom_size * parts * chunk, times), f32),
            pltpu.VMEM((DEPTH, 2, 2, UNROLL, lines, times), f32),
            pltpu.VMEM((units, 2, UNROLL, lines, times), f32),
            pltpu.VMEM((units, UNROLL, lines, times), f32),
            pltpu.VMEM((slots, 3, 2, times, full), f32),
            table,
            table,
            table,
            table,
            pltpu.VMEM((4, sites, times), f32),
            pltpu.VMEM((2, (STEPS + 1) * rows, times), f32),
            dma(()),
            dma((slots,)),
            dma((groups, mom_size)),
            dma((groups, mom_size)),
            dma((groups, pieces, mom_size)),
            dma((groups, pieces, mom_size)),
            dma((units,)),
            dma((units,)),
            dma((units,)),
            dma((units,)),
        ],
        compiler_params=pltpu.CompilerParams(
            collective_id=0, has_side_effects=True, vmem_limit_bytes=63 * 1024 * 1024
        ),
        name="advance_rows",
    )(momentum_map.reshape(1, -1), step_index, history_len, new_rows.reshape(flat), history)
    return result.reshape(new_rows.shape)


def solution(mesh):
    in_specs = (P(None, "mom", None, "tm"), P(None, None, "mom", "tm", None), P(), P(), P())
    out_specs = P(None, "mom", None, "tm")

    def dispatch(new_rows, *others):
        if fits(dict(mesh.shape), new_rows):
            return advance(mesh.shape["mom"], new_rows, *others)
        return body(new_rows, *others)

    return jax.shard_map(
        dispatch, mesh=mesh, in_specs=in_specs, out_specs=out_specs, check_vma=False
    )
```
